256 devices in a mesh: tm: 16 (over y_hi, z), tensor: 4 (over y_lo, core), dp: 4 (over x).
Axes of the slice: x: 4, y: 4 (y_hi: 2, y_lo: 2; y = y_hi * 2 + y_lo), z: 8, core: 2. Of those that a mesh axis runs over, the one named last changes fastest.
Arguments:
- video: bfloat16 [4, 16, 256, 1280], P('dp', 'tm'), may hold values from -6 to 6
- w_spatial: bfloat16 [3, 1280, 1280], P(None, 'dp', 'tensor'), as said below
- w_spatial_out: bfloat16 [1280, 1280], P('tensor', 'dp'), may hold values from -0.15625 to 0.15625
- temporal_weight: bfloat16 [3, 1280, 1280], P(None, 'dp', 'tensor'), as said below
- temporal_output_weight: bfloat16 [1280, 1280], P('tensor', 'dp'), may hold values from -0.15625 to 0.15625
- merger: bfloat16 [4, 1280, 8192], P(None, 'tensor', 'tm'), may hold values from -0.078125 to 0.078125
- text: bfloat16 [512, 8192], P('dp', 'tm'), may hold values from -6 to 6
- norm_gain: float32 [8192], P('tm'), may hold values from 0.1 to 1.9
- w_gate: bfloat16 [8192, 15360], P('tm', ('tensor', 'dp')), may hold values from -0.0625 to 0.0625
- w_up: bfloat16 [8192, 15360], P('tm', ('tensor', 'dp')), may hold values from -0.0625 to 0.0625
- w_down: bfloat16 [15360, 8192], P(('tensor', 'dp'), 'tm'), may hold values from -0.046875 to 0.046875
- probe: bfloat16 [512, 8192], P(None, 'tm'), may hold values from -0.25 to 0.25
- ref_margin: float32 [16], replicated, may hold values from -0.5 to 0.5
- pair_ids: int32 [512], replicated, may hold values from 0 to 3
- labels: int32 [512], replicated, may hold values from -1 to 1
- positions: int32 [512], P('dp'), may hold values from 0 to 1023
Outputs:
- losses: float32 [16], replicated
- grad_gate: bfloat16 [8192, 15360], P('tm', ('tensor', 'dp'))
- grad_up: bfloat16 [8192, 15360], P('tm', ('tensor', 'dp'))
- grad_down: bfloat16 [15360, 8192], P(('tensor', 'dp'), 'tm')
The draws below stay inside these ranges and needn't reach their ends.
Inputs may be any that keep to these rules, and one draw needn't show every extreme that they name: `w_spatial`: queries, keys and values in this order along the first dimension. `temporal_weight`: queries, keys and values in this order along the first dimension. `labels`: 1 for a chosen rollout's row, -1 for a rejected one's, 0 for a row outside the loss. `positions`: index f * 64 + g of the merged token, frame f and group g of four consecutive patches.
All inputs are finite; a program needn't handle non-finite values.
Results may differ from the reference program's by a relative error of at most 0.035.
Values may be sent and summed in bfloat16 or wider, within the bound.
No kernel may reach another device: no remote copies, remote signals or barrier semaphores. Data moves between devices by JAX's collectives and lax.ppermute only.
A program may use at most 128 MiB of HBM per device.

```python
import math
import jax
import jax.numpy as jnp
from jax import lax

W = 1280
HEADS = 16
P_SIZE = 256
F = 16
D = 8192
FF = 15360
ROWS = 128
R_ALL = 512
PAIRS_DEV = 4
PAIRS = 16
N_DP = 4


def drawn_projections(base_key):
    normal_draw = jax.random.normal(jax.random.fold_in(base_key, 11), (3, W, W), jnp.float32)
    return normal_draw / math.sqrt(W)


def draw_w_spatial(key, part):
    return drawn_projections(jax.random.fold_in(key, 101)).astype(jnp.bfloat16)


def draw_temporal_weight(key, part):
    return drawn_projections(jax.random.fold_in(key, 202)).astype(jnp.bfloat16)


def set_ends(values, rng, smallest, high):
    longest = values.shape.index(max(values.shape))
    spots = []
    for shift in (0, 1):
        where = [jax.random.randint(jax.random.fold_in(rng, axis), (), 0, length) for axis, length in enumerate(values.shape)]
        where[longest] = (where[longest] + shift) % values.shape[longest]
        spots.append(tuple(where))
    return values.at[spots[0]].set(smallest).at[spots[1]].set(high)


def shard_levels(own_key, shape, shards, least, high):
    loudness = 1.0
    for axis_at, shards_of in shards:
        steps = jax.random.uniform(jax.random.fold_in(jax.random.fold_in(own_key, 6), axis_at), (shards_of,), jnp.float32, least / len(shards), high / len(shards))
        loudness = loudness * jnp.repeat(jnp.exp(steps), shape[axis_at] // shards_of).reshape((-1,) + (1,) * (len(shape) - 1 - axis_at))
    return loudness


def scatter_about(key, extent, deviation, reach, shards=(), kind=jnp.bfloat16):
    factor_of = shard_levels(key, extent, shards, -0.22, 0.18) if shards else 1.0
    values = jax.random.normal(key, extent, jnp.float32) * deviation * factor_of
    return jnp.minimum(jnp.maximum(values, -reach), reach).astype(kind)


def setup_inputs(seed: int = 0) -> dict:
    streams_of = jax.random.split(jax.random.key(seed), 17)
    video = scatter_about(streams_of[0], (N_DP, F, P_SIZE, W), 1.0, 6.0, ((0, 4), (1, 16)))
    w_spatial = draw_w_spatial(jax.random.fold_in(streams_of[16], 71), 0)
    w_spatial_out = scatter_about(streams_of[2], (W, W), W ** -0.5, 0.15625, ((0, 4), (1, 4)))
    temporal_weight = draw_temporal_weight(jax.random.fold_in(streams_of[16], 71), 0)
    temporal_output_weight = scatter_about(streams_of[4], (W, W), W ** -0.5, 0.15625, ((0, 4), (1, 4)))
    merger = scatter_about(streams_of[5], (4, W, D), (4 * W) ** -0.5, 0.078125, ((1, 4), (2, 16)))
    text = scatter_about(streams_of[6], (R_ALL, D), 1.0, 6.0, ((0, 4), (1, 16)))
    norm_gain = jnp.clip(1.0 + 0.18 * jax.random.normal(streams_of[7], (D,), jnp.float32), 0.1, 1.9)
    w_gate = scatter_about(streams_of[8], (D, FF), D ** -0.5, 0.0625, ((0, 16), (1, 16)))
    w_up = scatter_about(streams_of[9], (D, FF), D ** -0.5, 0.0625, ((0, 16), (1, 16)))
    w_down = scatter_about(streams_of[10], (FF, D), FF ** -0.5, 0.046875, ((0, 16), (1, 16)))
    probe = scatter_about(streams_of[11], (R_ALL, D), (D // 16) ** -0.5, 0.25, ((1, 16),))
    ref_margin = jnp.clip(jax.random.uniform(streams_of[12], (PAIRS,), jnp.float32, -0.5, 0.5), -0.5, 0.5)
    pair_ids = set_ends(jax.random.randint(streams_of[13], (R_ALL,), 0, PAIRS_DEV), jax.random.fold_in(streams_of[13], 1), 0, PAIRS_DEV - 1).astype(jnp.int32)
    labels = set_ends(jax.random.randint(streams_of[14], (R_ALL,), -1, 2), jax.random.fold_in(streams_of[14], 1), -1, 1).astype(jnp.int32)
    positions = set_ends(jax.random.randint(streams_of[15], (R_ALL,), 0, F * P_SIZE // 4), jax.random.fold_in(streams_of[15], 1), 0, (F * P_SIZE // 4) - 1).astype(jnp.int32)
    return dict(video=video, w_spatial=w_spatial, w_spatial_out=w_spatial_out, temporal_weight=temporal_weight, temporal_output_weight=temporal_output_weight, merger=merger, text=text, norm_gain=norm_gain, w_gate=w_gate, w_up=w_up, w_down=w_down, probe=probe, ref_margin=ref_margin, pair_ids=pair_ids, labels=labels, positions=positions)


beta_scale = 0.1
loss_scale = 256.0
norm_eps = 1e-06

def layer_norm(values):
    centered = values - lax.optimization_barrier(jnp.mean(values, axis=-1, keepdims=True))
    spread = lax.optimization_barrier(jnp.mean(centered * centered, axis=-1, keepdims=True))
    return centered * lax.rsqrt(spread + norm_eps)

def attend(queries, key_rows, value_rows, head_size):
    leading = queries.shape[:-1]
    head_count = queries.shape[-1] // head_size

    def head_split(tensor_in):
        return tensor_in.astype(jnp.float32).reshape(tensor_in.shape[:-1] + (head_count, head_size))
    scores = jnp.einsum('...qhd,...khd->...hqk', head_split(queries), head_split(key_rows)) * head_size ** (-0.5)
    weights_soft = jax.nn.softmax(scores, axis=-1).astype(jnp.bfloat16)
    attended_context = jnp.einsum('...hqk,...khd->...qhd', weights_soft.astype(jnp.float32), head_split(value_rows))
    return attended_context.astype(jnp.bfloat16).reshape(leading + (head_count * head_size,))

def reference(video, w_spatial, w_spatial_out, temporal_weight, temporal_output_weight, merger, text, norm_gain, w_gate, w_up, w_down, probe, ref_margin, pair_ids, labels, positions):
    head_size = W // HEADS

    def spatial_frame(one_frame):
        normed_input = layer_norm(one_frame.astype(jnp.float32)).astype(jnp.bfloat16)
        query_slice = jnp.dot(normed_input, w_spatial[0], preferred_element_type=jnp.float32).astype(jnp.bfloat16)
        key_slice = jnp.dot(normed_input, w_spatial[1], preferred_element_type=jnp.float32).astype(jnp.bfloat16)
        value_slice = jnp.dot(normed_input, w_spatial[2], preferred_element_type=jnp.float32).astype(jnp.bfloat16)
        attended_context = attend(query_slice, key_slice, value_slice, head_size)
        return (one_frame.astype(jnp.float32) + jnp.dot(attended_context, w_spatial_out, preferred_element_type=jnp.float32)).astype(jnp.bfloat16)
    mixed = lax.map(spatial_frame, video.reshape(N_DP * F, P_SIZE, W)).reshape(N_DP, F, P_SIZE, W)

    def temporal_video(one_clip):
        normed_input = layer_norm(one_clip.astype(jnp.float32)).astype(jnp.bfloat16).astype(jnp.float32)
        query_slice = jnp.einsum('oly,yt->lot', normed_input, temporal_weight[0].astype(jnp.float32)).astype(jnp.bfloat16)
        key_slice = jnp.einsum('oly,yt->lot', normed_input, temporal_weight[1].astype(jnp.float32)).astype(jnp.bfloat16)
        value_slice = jnp.einsum('oly,yt->lot', normed_input, temporal_weight[2].astype(jnp.float32)).astype(jnp.bfloat16)
        attended_context = attend(query_slice, key_slice, value_slice, head_size)
        residual_update = jnp.einsum('lby,yd->bld', attended_context.astype(jnp.float32), temporal_output_weight.astype(jnp.float32))
        return (one_clip.astype(jnp.float32) + residual_update).astype(jnp.bfloat16)
    encoded = lax.map(temporal_video, mixed)
    per_video = F * (P_SIZE // 4)
    flat_tokens = encoded.reshape(N_DP * per_video, 4 * W)
    video_index = jnp.arange(R_ALL, dtype=jnp.int32) // ROWS
    picked = flat_tokens[(video_index * per_video + positions).astype(jnp.int32)]
    visual = jnp.dot(picked, merger.reshape(4 * W, D), preferred_element_type=jnp.float32)
    hidden_in = text.astype(jnp.float32) + visual
    mean_square = lax.optimization_barrier(jnp.mean(hidden_in * hidden_in, axis=1, keepdims=True))
    normed_rows = (hidden_in * lax.rsqrt(mean_square + norm_eps) * norm_gain[None, :]).astype(jnp.bfloat16)
    gate_pre = jnp.dot(normed_rows, w_gate, preferred_element_type=jnp.float32)
    up_pre = jnp.dot(normed_rows, w_up, preferred_element_type=jnp.float32)
    sig_gate = jax.nn.sigmoid(gate_pre)
    hidden = (gate_pre * sig_gate * up_pre).astype(jnp.bfloat16)
    delta = jnp.dot(hidden, w_down, preferred_element_type=jnp.float32)
    probe_wide = probe.astype(jnp.float32)
    score = lax.optimization_barrier(jnp.sum(delta * probe_wide, axis=1))
    global_pair = video_index * PAIRS_DEV + pair_ids
    member = (global_pair[:, None] == jnp.arange(PAIRS, dtype=jnp.int32)[None, :]).astype(jnp.float32)
    signed = labels.astype(jnp.float32)
    margin = jnp.dot(signed * score, member, precision=lax.Precision.HIGHEST)
    logits = beta_scale * margin - ref_margin
    losses = jax.nn.softplus(-logits)
    coefficient = -beta_scale * loss_scale * jax.nn.sigmoid(-logits)
    row_coef = jnp.dot(member, coefficient, precision=lax.Precision.HIGHEST) * signed
    cotangent = (row_coef[:, None] * probe_wide).astype(jnp.bfloat16)
    grad_down = jnp.dot(hidden.T, cotangent, preferred_element_type=jnp.float32).astype(jnp.bfloat16)
    hidden_grad = jnp.dot(cotangent, w_down.T, preferred_element_type=jnp.float32)
    gate_grad = (hidden_grad * up_pre * sig_gate * (1.0 + gate_pre * (1.0 - sig_gate))).astype(jnp.bfloat16)
    up_grad = (hidden_grad * gate_pre * sig_gate).astype(jnp.bfloat16)
    grad_gate = jnp.dot(normed_rows.T, gate_grad, preferred_element_type=jnp.float32).astype(jnp.bfloat16)
    grad_up = jnp.dot(normed_rows.T, up_grad, preferred_element_type=jnp.float32).astype(jnp.bfloat16)
    return (losses, grad_gate, grad_up, grad_down)
```

```python
import functools

import jax
import jax.numpy as jnp
from jax import lax
from jax.experimental import pallas as pl
from jax.experimental.pallas import tpu as pltpu
from jax.sharding import Mesh
from jax.sharding import PartitionSpec as P


HEADS = 16
PAIRS_DEV = 4
TENSOR = ("tensor_0", "tensor_1")
TM = ("tm_0", "tm_1")
TENSOR_DP = ("tensor_0", "tensor_1", "dp")
F32 = jnp.float32
BF16 = jnp.bfloat16

beta_scale = 0.1
loss_scale = 256.0
norm_eps = 1e-06
LOW = -1e30

VM = pl.BlockSpec(memory_space=pltpu.VMEM)
SM = pl.BlockSpec(memory_space=pltpu.SMEM)
HB = pl.BlockSpec(memory_space=pl.ANY)


def shape_of(shape, dtype=BF16):
    return jax.ShapeDtypeStruct(shape, dtype)


def dot(a, b):
    return jnp.dot(a, b, preferred_element_type=F32)


def dot_rows(a, b):
    return lax.dot_general(a, b, (((1,), (1,)), ((), ())), preferred_element_type=F32)


def dot_down(a, b):
    return lax.dot_general(a, b, (((0,), (0,)), ((), ())), preferred_element_type=F32)


def head_masks(width, size):
    lane = lax.broadcasted_iota(jnp.int32, (1, width), 1)
    return [
        jnp.where((lane >= h * size) & (lane < (h + 1) * size), 1.0, 0.0).astype(BF16)
        for h in range(width // size)
    ]


def run(kernel, out_shape, in_specs, args, scratch=(), cost=(0, 0)):
    outs = jax.tree.map(lambda _: VM, out_shape)
    return pl.pallas_call(
        kernel,
        out_shape=out_shape,
        in_specs=in_specs,
        out_specs=outs,
        scratch_shapes=list(scratch),
        compiler_params=pltpu.CompilerParams(vmem_limit_bytes=60000 * 1024),
        cost_estimate=pl.CostEstimate(flops=cost[0], bytes_accessed=cost[1], transcendentals=0),
    )(*args)


def probe_kernel(zs, ys, probe_ref, w_ref, out_ref):
    part = out_ref.shape[1]
    for z in range(zs):
        rows = probe_ref[z * ys * part : (z + 1) * ys * part]
        pd = dot_rows(rows, w_ref[...]).astype(BF16)
        for y in range(ys):
            out_ref[y * zs + z] = pd[y * part : (y + 1) * part]


def spatial_kernel(size, dp_ref, x_ref, w_ref, o0, o1, o2, o3, out_ref, w_all):
    blocks, _, depth, width = w_ref.shape
    x = x_ref[...].astype(F32)
    x = x - jnp.mean(x, axis=-1, keepdims=True)
    xs = (x * lax.rsqrt(jnp.mean(x * x, axis=-1, keepdims=True) + norm_eps)).astype(BF16)
    proj = []
    for j in range(3):
        for d in range(blocks):
            w_all[j, d * depth : (d + 1) * depth] = w_ref[d, j]
        proj.append(dot(xs, w_all[j]).astype(BF16))
    q, k, v = proj
    ctx = jnp.zeros(q.shape, F32)
    for mask in head_masks(width, size):
        s = dot_rows(q * mask, k) * size ** (-0.5)
        e = jnp.exp(s - jnp.max(s, axis=-1, keepdims=True))
        p = (e / jnp.sum(e, axis=-1, keepdims=True)).astype(BF16)
        ctx = ctx + dot(p, v * mask)
    ctx = ctx.astype(BF16)
    for s, o in enumerate((o0, o1, o2, o3)):
        out_ref[dp_ref[0] ^ s] = dot(ctx, o[...]).astype(BF16)


def pick_kernel(parts_ref, own_ref, idx_ref, out_ref):
    hs = own_ref[...].astype(F32)
    for s in range(parts_ref.shape[0]):
        hs = hs + parts_ref[s].astype(F32)
    hs = hs.astype(BF16)
    token = lax.broadcasted_iota(jnp.int32, (idx_ref.shape[0], hs.shape[0]), 1)
    hit = jnp.where(token == idx_ref[...], 1.0, 0.0).astype(BF16)
    got = dot(hit, hs).astype(BF16)
    rows = out_ref.shape[1]
    for t in range(out_ref.shape[0]):
        out_ref[t] = got[t * rows : (t + 1) * rows]


def temporal_kernel(size, te_ref, x0, x1, x2, x3, w_ref, o_ref, frame_ref, out_ref, own_ref):
    te = te_ref[0]
    xs = [x0[...], x1[...], x2[...], x3[...]]
    n = len(xs)
    rows, width = xs[0].shape
    toks = frame_ref.shape[0]
    wide = [x.astype(F32) for x in xs]
    mean = sum(jnp.sum(x, axis=-1, keepdims=True) for x in wide) / (n * width)
    wide = [x - mean for x in wide]
    var = sum(jnp.sum(x * x, axis=-1, keepdims=True) for x in wide) / (n * width)
    scale = lax.rsqrt(var + norm_eps)
    xt = [(x * scale).astype(BF16) for x in wide]
    row = lax.broadcasted_iota(jnp.int32, (toks, rows), 1)
    tok = lax.broadcasted_iota(jnp.int32, (toks, rows), 0)
    sel = jnp.where(row == frame_ref[...] * toks + tok, 1.0, 0.0).astype(BF16)
    own_ref[...] = dot(sel, xs[0]).astype(BF16)
    q = sum(dot(dot(sel, xt[s]).astype(BF16), w_ref[te ^ s, 0]) for s in range(n)).astype(BF16)
    k = sum(dot(xt[s], w_ref[te ^ s, 1]) for s in range(n)).astype(BF16)
    v = sum(dot(xt[s], w_ref[te ^ s, 2]) for s in range(n)).astype(BF16)
    same = lax.rem(row, toks) == tok
    ctx = jnp.zeros((toks, width), F32)
    for mask in head_masks(width, size):
        s = jnp.where(same, dot_rows(q * mask, k) * size ** (-0.5), LOW)
        e = jnp.where(same, jnp.exp(s - jnp.max(s, axis=-1, keepdims=True)), 0.0)
        p = (e / jnp.sum(e, axis=-1, keepdims=True)).astype(BF16)
        ctx = ctx + dot(p, v * mask)
    ctx = ctx.astype(BF16)
    for d in range(n):
        out_ref[d] = dot(ctx, o_ref[d]).astype(BF16)


def merge_kernel(x_ref, w_ref, out_ref):
    quads = w_ref.shape[0]
    rows = out_ref.shape[0]
    x = x_ref[...]
    r = lax.broadcasted_iota(jnp.int32, (rows, x.shape[0]), 0)
    t = lax.broadcasted_iota(jnp.int32, (rows, x.shape[0]), 1)
    total = jnp.zeros(out_ref.shape, F32)
    for q in range(quads):
        sel = jnp.where(t == r * quads + q, 1.0, 0.0).astype(BF16)
        total = total + dot(dot(sel, x).astype(BF16), w_ref[q])
    out_ref[...] = total.astype(BF16)


def gate_kernel(dp_ref, u0, u1, u2, u3, wg_ref, wu_ref, out_ref, all_ref):
    rows = u0.shape[0]
    part = out_ref.shape[2]
    per = rows // part
    for s, u in enumerate((u0, u1, u2, u3)):
        b = dp_ref[0] ^ s
        x = u[...]
        all_ref[pl.ds(pl.multiple_of(b * rows, rows), rows), :] = x
        for j, w in enumerate((wg_ref, wu_ref)):
            y = dot(x, w[...]).astype(BF16)
            for h in range(per):
                out_ref[b * per + h, j] = y[h * part : (h + 1) * part]


def grad_kernel(gu_ref, pd_ref, inv_ref, rc_ref, act_ref, probe_ref, gg_ref, gup_ref, gd_ref, hid, dg, du):
    part = gu_ref.shape[2]
    for z in range(gu_ref.shape[0]):
        at = slice(z * part, (z + 1) * part)
        inv = inv_ref[at]
        gate = gu_ref[z, 0].astype(F32) * inv
        up = gu_ref[z, 1].astype(F32) * inv
        sg = jax.nn.sigmoid(gate)
        dh = pd_ref[at].astype(F32) * rc_ref[at]
        hid[at] = (gate * sg * up).astype(BF16)
        dg[at] = (dh * up * sg * (1.0 + gate * (1.0 - sg)) * inv).astype(BF16)
        du[at] = (dh * gate * sg * inv).astype(BF16)
    act = act_ref[...]
    gg_ref[...] = dot_down(act, dg[...]).astype(BF16)
    gup_ref[...] = dot_down(act, du[...]).astype(BF16)
    cot = (rc_ref[...] * probe_ref[...].astype(F32)).astype(BF16)
    gd_ref[...] = dot_down(hid[...], cot).astype(BF16)


def swaps(x, axis, size):
    return [x] + [
        lax.ppermute(x, axis, [(k, k ^ s) for k in range(size)]) for s in range(1, size)
    ]


def sent_to_all(x, axis):
    size = lax.axis_size(axis)
    return lax.all_to_all(jnp.broadcast_to(x[None], (size, *x.shape)), axis, 0, 0, tiled=True)


def body(
    video,
    w_spatial,
    w_spatial_out,
    temporal_weight,
    temporal_output_weight,
    merger,
    text,
    norm_gain,
    w_gate,
    w_up,
    w_down,
    probe,
    ref_margin,
    pair_ids,
    labels,
    positions,
):
    te_n = lax.axis_size(TENSOR)
    dp_n = lax.axis_size("dp")
    tm_n = lax.axis_size(TM)
    z_n = lax.axis_size("tm_1")
    y_n = lax.axis_size("tm_0")
    te = lax.axis_index(TENSOR)
    dp = lax.axis_index("dp")
    tm = lax.axis_index(TM)
    y_at = lax.axis_index("tm_0")
    z_at = lax.axis_index("tm_1")
    te_s = te.astype(jnp.int32).reshape(1)
    dp_s = dp.astype(jnp.int32).reshape(1)

    frame = video[0, 0]
    patches, width = frame.shape
    size = width // HEADS
    own_w = width // te_n
    rows = positions.shape[0]
    total_rows = probe.shape[0]
    hid = w_gate.shape[1]
    own_rows = rows // tm_n
    toks = own_rows * 4
    chunk = total_rows // z_n
    model = norm_gain.shape[0] * tm_n

    w4 = lax.all_gather(w_spatial, "dp")
    wo = swaps(w_spatial_out, "dp", dp_n)
    w4t = lax.all_gather(temporal_weight, "dp")
    w4o = lax.all_gather(temporal_output_weight, "dp")

    pd_part = run(
        functools.partial(probe_kernel, z_n, y_n),
        shape_of((tm_n, total_rows // tm_n, hid)),
        [VM, VM],
        (probe, w_down),
        cost=(2 * total_rows * hid * probe.shape[1], 3 << 20),
    )
    pd_got = lax.all_to_all(pd_part, TM, 0, 0, tiled=True)
    pd_own = pd_got.astype(F32).sum(axis=0).astype(BF16)
    pd_other = lax.ppermute(pd_own, "tm_0", [(0, 1), (1, 0)])
    first = jnp.where(y_at == 0, pd_own, pd_other)
    second = jnp.where(y_at == 0, pd_other, pd_own)
    pd_chunk = jnp.concatenate([first, second], axis=0)
    pd_all = lax.all_gather(pd_chunk, "tm_1", axis=0, tiled=True)

    parts = run(
        functools.partial(spatial_kernel, size),
        shape_of((te_n, patches, own_w)),
        [SM] + [VM] * 6,
        (dp_s, frame, w4, *wo),
        scratch=[pltpu.VMEM((3, width, own_w), BF16)],
        cost=(2 * patches * width * own_w * 5, 5 << 20),
    )
    parts = lax.all_to_all(parts, TENSOR, 0, 0, tiled=True)

    own_frame = lax.dynamic_slice_in_dim(frame, te * own_w, own_w, 1)
    group = positions % (patches // 4)
    token = (group[:, None] * 4 + jnp.arange(4, dtype=jnp.int32)[None, :]).reshape(rows * 4, 1)
    taken = run(
        pick_kernel,
        shape_of((tm_n, toks, own_w)),
        [VM] * 3,
        (parts, own_frame, token),
        cost=(2 * rows * 4 * patches * own_w, 2 << 20),
    )
    taken = lax.all_to_all(taken, TM, 0, 0, tiled=True)
    columns = swaps(taken.reshape(tm_n * toks, own_w), TENSOR, te_n)

    own_pos = lax.dynamic_slice_in_dim(positions, tm * own_rows, own_rows, 0)
    frame_of = jnp.broadcast_to((own_pos // (patches // 4))[:, None], (own_rows, 4)).reshape(toks, 1)
    t_parts, own_tok = run(
        functools.partial(temporal_kernel, size),
        (shape_of((te_n, toks, own_w)), shape_of((toks, own_w))),
        [SM] + [VM] * 7,
        (te_s, *columns, w4t, w4o, frame_of),
        cost=(2 * tm_n * toks * width * own_w * 2, 5 << 20),
    )
    t_parts = lax.all_to_all(t_parts, TENSOR, 0, 0, tiled=True)
    enc = (own_tok.astype(F32) + t_parts.astype(F32).sum(axis=0)).astype(BF16)
    picked = sent_to_all(enc, TM).reshape(tm_n * toks, own_w)

    vis = run(
        merge_kernel,
        shape_of((rows, merger.shape[2])),
        [VM] * 2,
        (picked, merger),
        cost=(2 * rows * 4 * own_w * merger.shape[2], 2 << 20),
    )
    vis = swaps(vis, TENSOR, te_n)
    u = text.astype(F32) + sum(v.astype(F32) for v in vis)
    ug = (u * norm_gain[None, :]).astype(BF16)
    square = jnp.sum(u * u, axis=1)
    ug4 = swaps(ug, "dp", dp_n)

    gu, act = run(
        gate_kernel,
        (shape_of((z_n, 2, chunk, hid)), shape_of((total_rows, ug.shape[1]))),
        [SM] + [VM] * 6,
        (dp_s, *ug4, w_gate, w_up),
        cost=(4 * total_rows * hid * ug.shape[1], 6 << 20),
    )
    gu = lax.psum_scatter(gu.reshape(z_n * 2 * chunk, hid), "tm_1", scatter_dimension=0, tiled=True)
    gu_other = lax.ppermute(gu, "tm_0", [(0, 1), (1, 0)])
    gu = (gu.astype(F32) + gu_other.astype(F32)).astype(BF16)
    gu_all = lax.all_gather(gu.reshape(2, chunk, hid), "tm_1")

    square = sent_to_all(square.reshape(1, rows), "dp").reshape(1, total_rows)
    square = sent_to_all(square, TM).reshape(tm_n, total_rows).sum(axis=0)
    inv = lax.rsqrt(square / model + norm_eps)[:, None]

    pair_total = ref_margin.shape[0]
    global_pair = jnp.arange(total_rows, dtype=jnp.int32) // rows * PAIRS_DEV + pair_ids
    member = (global_pair[:, None] == jnp.arange(pair_total, dtype=jnp.int32)[None, :]).astype(F32)
    signed = member * labels.astype(F32)[:, None]
    own_inv = lax.dynamic_slice_in_dim(inv, z_at * chunk, chunk, 0)
    own_signed = lax.dynamic_slice_in_dim(signed, z_at * chunk, chunk, 0)
    gate = gu[:chunk].astype(F32) * own_inv
    up = gu[chunk:].astype(F32) * own_inv
    hidden = (gate * jax.nn.sigmoid(gate) * up).astype(BF16).astype(F32)
    score = jnp.sum(hidden * pd_chunk.astype(F32), axis=1, keepdims=True)
    margin = jnp.sum(score * own_signed, axis=0, keepdims=True)
    for axis in (TENSOR, "dp", "tm_1"):
        margin = sent_to_all(margin, axis).reshape(-1, pair_total).sum(axis=0, keepdims=True)
    logits = beta_scale * margin[0] - ref_margin
    losses = jax.nn.softplus(-logits)
    coefficient = -beta_scale * loss_scale * jax.nn.sigmoid(-logits)
    row_coef = jnp.sum(signed * coefficient[None, :], axis=1, keepdims=True)

    gg, gup, gd = run(
        grad_kernel,
        (shape_of((ug.shape[1], hid)), shape_of((ug.shape[1], hid)), shape_of((hid, probe.shape[1]))),
        [VM] * 6,
        (gu_all, pd_all, inv, row_coef, act, probe),
        scratch=[pltpu.VMEM((total_rows, hid), BF16)] * 3,
        cost=(6 * total_rows * hid * ug.shape[1], 8 << 20),
    )
    return (losses, gg, gup, gd)


def solution(mesh):
    finer = Mesh(
        mesh.devices.reshape(2, 8, 2, 2, mesh.shape["dp"]),
        ("tm_0", "tm_1", "tensor_0", "tensor_1", "dp"),
    )
    return jax.shard_map(
        body,
        mesh=finer,
        in_specs=(
            P("dp", TM, None, None),
            P(None, "dp", TENSOR),
            P(TENSOR, "dp"),
            P(None, "dp", TENSOR),
            P(TENSOR, "dp"),
            P(None, TENSOR, TM),
            P("dp", TM),
            P(TM),
            P(TM, TENSOR_DP),
            P(TM, TENSOR_DP),
            P(TENSOR_DP, TM),
            P(None, TM),
            P(),
            P(),
            P(),
            P("dp"),
        ),
        out_specs=(P(), P(TM, TENSOR_DP), P(TM, TENSOR_DP), P(TENSOR_DP, TM)),
        check_vma=False,
    )
```
